32 devices in a mesh: rep: 16 (over z, y, core), shard: 2 (over x).
Axes of the slice: x: 2, y: 2, z: 4, core: 2. Of those that a mesh axis runs over, the one named last changes fastest.
Arguments:
- tokens: bfloat16 [32768, 768], P(('rep', 'shard')), may hold values from -6 to 6
- image_ids: int32 [32, 1024], P(('rep', 'shard')), may hold values from 0 to 7, never falling along the last dimension, each value on 1 to 256 neighbouring positions
- ln1_gain: bfloat16 [768], P('shard'), may hold values from 0.5 to 1.5
- ln1_bias: bfloat16 [768], P('shard'), may hold values from -3 to 3
- w_query: bfloat16 [768, 768], P('shard'), may hold values from -0.21875 to 0.21875
- w_key: bfloat16 [768, 768], P('shard'), may hold values from -0.21875 to 0.21875
- w_value: bfloat16 [768, 768], P('shard'), may hold values from -0.21875 to 0.21875
- b_value: bfloat16 [768], P('shard'), may hold values from -3 to 3
- q_gain: bfloat16 [768], P('shard'), may hold values from 0.796875 to 1.59375
- k_gain: bfloat16 [768], P('shard'), may hold values from 0.796875 to 1.59375
- w_out: bfloat16 [768, 768], P('shard'), may hold values from -0.875 to 0.875
- b_out: bfloat16 [768], P('shard'), may hold values from -3 to 3
- ln2_gain: bfloat16 [768], P('shard'), may hold values from 0.5 to 1.5
- ln2_bias: bfloat16 [768], P('shard'), may hold values from -3 to 3
- w_up: bfloat16 [768, 3072], P('shard'), may hold values from -0.21875 to 0.21875
- b_up: bfloat16 [3072], P('shard'), may hold values from -3 to 3
- w_down: bfloat16 [3072, 768], P('shard'), may hold values from -0.15625 to 0.15625
- b_down: bfloat16 [768], P('shard'), may hold values from -3 to 3
- cotangent: bfloat16 [32768, 768], P(('rep', 'shard')), may hold values from -6 to 6
Outputs:
- outputs: bfloat16 [32768, 768], P(('rep', 'shard'))
- d_tokens: bfloat16 [32768, 768], P(('rep', 'shard'))
- g_ln1_gain: float32 [768], P('shard')
- g_ln1_bias: float32 [768], P('shard')
- g_w_query: float32 [768, 768], P('shard')
- g_w_key: float32 [768, 768], P('shard')
- g_w_value: float32 [768, 768], P('shard')
- g_b_value: float32 [768], P('shard')
- g_q_gain: float32 [768], P('shard')
- g_k_gain: float32 [768], P('shard')
- g_w_out: float32 [768, 768], P('shard')
- g_b_out: float32 [768], P('shard')
- g_ln2_gain: float32 [768], P('shard')
- g_ln2_bias: float32 [768], P('shard')
- g_w_up: float32 [768, 3072], P('shard')
- g_b_up: float32 [3072], P('shard')
- g_w_down: float32 [3072, 768], P('shard')
- g_b_down: float32 [768], P('shard')
The draws below stay inside these ranges and needn't reach their ends.
Inputs may be any that keep to these rules, and one draw needn't show every extreme that they name: `image_ids`: each row is one packed sequence: ids never fall along the row, each image has 1 to 256 tokens, one exactly 256, and a row holds 8 images.
All inputs are finite; a program needn't handle non-finite values.
Results may differ from the reference program's by a relative error of at most 0.012.
Values may be sent and summed in bfloat16 or wider, within the bound.
A program may use at most 192 MiB of HBM per device.

```python
import math
import jax
import jax.numpy as jnp
import numpy as np
from jax import lax

D = 768
HEADS = 12
FF = 3072
TOK_DEV = 1024
IMG_MOST = 256
IMG_SEQ = 8
SEQS = 32
TOKENS = 32768


def block_levels(stream_key, shape, pieces, least, top_value):
    loudness = 1.0
    for axis_at, parts in pieces:
        draws = jax.random.uniform(jax.random.fold_in(jax.random.fold_in(stream_key, 6), axis_at), (parts,), jnp.float32, least / len(pieces), top_value / len(pieces))
        loudness = loudness * jnp.repeat(jnp.exp(draws), shape[axis_at] // parts).reshape((-1,) + (1,) * (len(shape) - 1 - axis_at))
    return loudness


def profile(count, total, most, lean):
    loads = [(1 << 20) // math.isqrt(grade ** lean) + 1 for grade in range(2, count + 1)]
    rest, counts = total - most - (count - 1), [1] * (count - 1)
    while rest > 0:
        movable = [i for i in range(count - 1) if counts[i] < most]
        mass, budget = sum([loads[i] for i in movable]), rest
        for i in movable:
            more = min(most - counts[i], max(1, budget * loads[i] // mass), rest)
            counts[i] = counts[i] + more
            rest = rest - more
    return np.array([most] + counts)


def uneven(stream_key, number_of, total, reach, skew):
    if number_of == 2:
        one = jax.random.randint(stream_key, (), max(1, total - reach), min(reach, total - 1) + 1)
        return jnp.stack([one, total - one])
    lengths = jnp.asarray(profile(number_of, total, reach, skew), jnp.int32)
    pairs = (number_of - 1) // 2
    donor, receiver = lengths[1:1 + 2 * pairs:2], lengths[2:2 + 2 * pairs:2]
    margin = jnp.minimum(donor - 1, reach - receiver)
    shifted = jax.random.randint(jax.random.fold_in(stream_key, 1), (pairs,), 0, 1 << 20) % (margin + 1)
    lengths = lengths.at[1:1 + 2 * pairs:2].set(donor - shifted).at[2:2 + 2 * pairs:2].set(receiver + shifted)
    return lengths[jax.random.permutation(jax.random.fold_in(stream_key, 2), number_of)]


def scatter_about(rng, dims, scale, most, cuts=(), held_as=jnp.bfloat16):
    level = block_levels(rng, dims, cuts, -0.22, 0.18) if cuts else 1.0
    values = jax.random.normal(rng, dims, jnp.float32) * scale * level
    return jnp.minimum(jnp.maximum(values, -most), most).astype(held_as)


def setup_inputs(seed: int = 0) -> dict:
    key_of = jax.random.split(jax.random.key(seed), 20)
    return {
        "tokens": scatter_about(key_of[0], (TOKENS, D), 1.0, 6.0, ((0, 32),)),
        "image_ids": jax.vmap(lambda own: jnp.searchsorted(jnp.cumsum(uneven(own, IMG_SEQ, TOK_DEV, IMG_MOST, 2)), jnp.arange(TOK_DEV), side="right"))(jax.random.split(key_of[1], SEQS)).reshape((SEQS, TOK_DEV)).astype(jnp.int32),
        "ln1_gain": jnp.clip(0.5 + 1.0 * jax.random.uniform(key_of[2], (D,), jnp.float32) ** block_levels(key_of[2], (D,), ((0, 2),), -0.2, 0.2), 0.5, 1.5).astype(jnp.bfloat16),
        "ln1_bias": scatter_about(key_of[3], (D,), 0.5, 3.0, ((0, 2),)),
        "w_query": scatter_about(key_of[4], (D, D), D ** -0.5, 0.21875, ((0, 2),)),
        "w_key": scatter_about(key_of[5], (D, D), D ** -0.5, 0.21875, ((0, 2),)),
        "w_value": scatter_about(key_of[6], (D, D), D ** -0.5, 0.21875, ((0, 2),)),
        "b_value": scatter_about(key_of[7], (D,), 0.5, 3.0, ((0, 2),)),
        "q_gain": jnp.clip(0.796875 + 0.796875 * jax.random.uniform(key_of[8], (D,), jnp.float32) ** block_levels(key_of[8], (D,), ((0, 2),), -0.2, 0.2), 0.796875, 1.59375).astype(jnp.bfloat16),
        "k_gain": jnp.clip(0.796875 + 0.796875 * jax.random.uniform(key_of[9], (D,), jnp.float32) ** block_levels(key_of[9], (D,), ((0, 2),), -0.2, 0.2), 0.796875, 1.59375).astype(jnp.bfloat16),
        "w_out": scatter_about(key_of[10], (D, D), (D // 16) ** -0.5, 0.875, ((0, 2),)),
        "b_out": scatter_about(key_of[11], (D,), 0.5, 3.0, ((0, 2),)),
        "ln2_gain": jnp.clip(0.5 + 1.0 * jax.random.uniform(key_of[12], (D,), jnp.float32) ** block_levels(key_of[12], (D,), ((0, 2),), -0.2, 0.2), 0.5, 1.5).astype(jnp.bfloat16),
        "ln2_bias": scatter_about(key_of[13], (D,), 0.5, 3.0, ((0, 2),)),
        "w_up": scatter_about(key_of[14], (D, FF), D ** -0.5, 0.21875, ((0, 2),)),
        "b_up": scatter_about(key_of[15], (FF,), 0.5, 3.0, ((0, 2),)),
        "w_down": scatter_about(key_of[16], (FF, D), (FF // 2) ** -0.5, 0.15625, ((0, 2),)),
        "b_down": scatter_about(key_of[17], (D,), 0.5, 3.0, ((0, 2),)),
        "cotangent": scatter_about(key_of[18], (TOKENS, D), 1.0, 6.0, ((0, 32),)),
    }


@jax.custom_vjp
def low(v):
    return lax.optimization_barrier(v.astype(jnp.bfloat16)).astype(jnp.float32)

@jax.custom_vjp
def low_back(v):
    return v

def low_keep(v):
    return (low(v), None)

def low_pass(kept, grad):
    return (grad,)

def back_keep(v):
    return (v, None)

def back_low(kept, grad):
    return (low(grad),)
low.defvjp(low_keep, low_pass)
low_back.defvjp(back_keep, back_low)
EPS = 1e-06
HIGH = lax.Precision.HIGHEST

def matmul(left, right):
    return jnp.dot(left, right, precision=HIGH)

def norm_rows(value, gain, bias):
    centre = value - lax.optimization_barrier(jnp.mean(value, -1, keepdims=True))
    spread = lax.optimization_barrier(jnp.mean(centre * centre, -1, keepdims=True))
    return centre * lax.rsqrt(spread + EPS) * gain + bias

def norm_heads(value, gain):
    rows = value.shape[0]
    split = value.reshape(rows, HEADS, D // HEADS)
    centre = split - lax.optimization_barrier(jnp.mean(split, -1, keepdims=True))
    spread = lax.optimization_barrier(jnp.mean(centre * centre, -1, keepdims=True))
    return (centre * lax.rsqrt(spread + EPS)).reshape(rows, D) * gain

def forward(weights, rows_in, ids):
    ln1_gain, ln1_bias, w_query, w_key, w_value, b_value, q_gain, k_gain, w_out, b_out, ln2_gain, ln2_bias, w_up, b_up, w_down, b_down = weights
    count = rows_in.shape[0]
    scale = 1.0 / math.sqrt(D // HEADS)
    h_one = low(norm_rows(rows_in, ln1_gain, ln1_bias))
    q_raw = low_back(matmul(h_one, w_query))
    k_raw = low_back(matmul(h_one, w_key))
    values = low(low_back(matmul(h_one, w_value) + b_value))
    query = low(norm_heads(q_raw, q_gain)).reshape(count, HEADS, D // HEADS)
    key = low(norm_heads(k_raw, k_gain)).reshape(count, HEADS, D // HEADS)
    values = values.reshape(count, HEADS, D // HEADS)
    scores = low_back(jnp.einsum('qhd,khd->hqk', query, key, precision=HIGH) * scale)
    allowed = ids[:, None] == ids[None, :]
    scores = jnp.where(allowed[None], scores, -1e+30)
    probs = low(jax.nn.softmax(scores, axis=-1))
    context = low(low_back(jnp.einsum('hqk,khd->qhd', probs, values, precision=HIGH)))
    context = context.reshape(count, D)
    attended = low_back(matmul(context, w_out) + b_out)
    x_one = rows_in + attended
    h_two = low(norm_rows(x_one, ln2_gain, ln2_bias))
    pre = low_back(matmul(h_two, w_up) + b_up)
    act = low(jax.nn.gelu(pre, approximate=False))
    branch = low_back(matmul(act, w_down) + b_down)
    return x_one + branch

def reference(tokens, image_ids, ln1_gain, ln1_bias, w_query, w_key, w_value, b_value, q_gain, k_gain, w_out, b_out, ln2_gain, ln2_bias, w_up, b_up, w_down, b_down, cotangent):
    weights = tuple((w.astype(jnp.float32) for w in (ln1_gain, ln1_bias, w_query, w_key, w_value, b_value, q_gain, k_gain, w_out, b_out, ln2_gain, ln2_bias, w_up, b_up, w_down, b_down)))
    seq_rows = tokens.astype(jnp.float32).reshape(SEQS, TOK_DEV, D)
    seq_cot = cotangent.astype(jnp.float32).reshape(SEQS, TOK_DEV, D)

    def one_seq(totals, items):
        rows_in, ids, cot = items

        def apply(*values):
            return forward(values[:-1], values[-1], ids)
        result, pull = jax.vjp(apply, *weights, rows_in)
        grads = pull(cot)
        totals = tuple((t + g for t, g in zip(totals, grads[:-1])))
        return (totals, (result.astype(jnp.bfloat16), grads[-1].astype(jnp.bfloat16)))
    zeros = tuple((jnp.zeros(w.shape, jnp.float32) for w in weights))
    totals, (results, d_rows) = lax.scan(one_seq, zeros, (seq_rows, image_ids, seq_cot))
    return (results.reshape(TOKENS, D), d_rows.reshape(TOKENS, D), totals[0], totals[1], totals[2], totals[3], totals[4], totals[5], totals[6], totals[7], totals[8], totals[9], totals[10], totals[11], totals[12], totals[13], totals[14], totals[15])
```

```python
import functools
import math

import jax
import jax.numpy as jnp
from jax import lax
from jax.experimental import pallas as pl
from jax.experimental.pallas import tpu as pltpu
from jax.sharding import PartitionSpec as P

T = 1024
D = 768
FF = 3072
HEADS = 12
DH = D // HEADS
EPS = 1e-06
SCALE = 1.0 / math.sqrt(DH)
RSQRT2 = math.sqrt(0.5)
RSQRT2PI = 1.0 / math.sqrt(2.0 * math.pi)

HD = D // 2
HF = FF // 2
NJ = 6
FC = FF // NJ
FH = FC // 2
RB = 256
NR = T // RB
KB = 256
NK = T // KB

VEC = dict(
    ln1_gain=0,
    ln1_bias=1 * HD,
    b_value=2 * HD,
    q_gain=3 * HD,
    k_gain=4 * HD,
    b_out=5 * HD,
    ln2_gain=6 * HD,
    ln2_bias=7 * HD,
    b_down=8 * HD,
    b_up=9 * HD,
)
NV = 9 * HD + HF

f32 = jnp.float32
bf16 = jnp.bfloat16
MESH = pl.DeviceIdType.MESH


def dot(left, right, cl, cr):
    return lax.dot_general(left, right, (((cl,), (cr,)), ((), ())), preferred_element_type=f32)


def rows_loop(body):
    def step(r, carry):
        body(pl.ds(pl.multiple_of(r * RB, RB), RB))
        return carry

    lax.fori_loop(0, NR, step, 0)


def head_mean(value, avg):
    high = value.astype(bf16)
    low = (value - high.astype(f32)).astype(bf16)
    return dot(high, avg, 1, 0) + dot(low, avg, 1, 0)


def row_stats(value):
    centre = value - jnp.mean(value, -1, keepdims=True)
    spread = jnp.mean(centre * centre, -1, keepdims=True)
    inv = lax.rsqrt(spread + EPS)
    return centre * inv, inv


def vector(vec, name):
    at = VEC[name]
    return jnp.concatenate([vec[0, :, at : at + HD], vec[1, :, at : at + HD]], 1)


def add_vector(gvec, name, total):
    at = VEC[name]
    gvec[0, :, at : at + HD] += total[:, :HD]
    gvec[1, :, at : at + HD] += total[:, HD:]


def col_sum(value):
    return jnp.sum(value, 0, keepdims=True)


class Plain:
    def __init__(self, ins, outs, refs):
        self.ins, self.outs, self.refs = ins, outs, refs

    def begin(self):
        i, r, sem = self.ins, self.refs, self.refs["load_sem"]
        pairs = [(i[n], r["w4"].at[k]) for k, n in enumerate(("w_query", "w_key", "w_value", "w_out"))]
        for j in range(NJ):
            for h in range(2):
                pairs.append((i["w_up"].at[:, pl.ds(h * HF + j * FH, FH)], r["wup"].at[j, :, pl.ds(h * FH, FH)]))
                pairs.append((i["w_down"].at[pl.ds(h * HF + j * FH, FH), :], r["wdn"].at[j, pl.ds(h * FH, FH), :]))
        pairs.append((i["vec"], r["vec"]))
        copies = [pltpu.make_async_copy(a, b, sem.at[k]) for k, (a, b) in enumerate(pairs)]
        for c in copies:
            c.start()
        for c in copies:
            c.wait()

    def weights(self, point, j=None):
        pass

    def put(self, pairs):
        copies = [pltpu.make_async_copy(a, b, self.refs["load_sem"].at[k]) for k, (a, b) in enumerate(pairs)]
        for c in copies:
            c.start()
        for c in copies:
            c.wait()

    def emit_mlp(self, j, up, down):
        gu, gd, o = self.refs["g_up"], self.refs["g_dn"], self.outs
        gu[0] = up()
        gd[0] = down()
        pairs = []
        for h in range(2):
            at = pl.multiple_of(h * HF + j * FH, FH)
            pairs.append((gu.at[0, :, pl.ds(h * FH, FH)], o["g_up"].at[:, pl.ds(at, FH)]))
            pairs.append((gd.at[0, pl.ds(h * FH, FH), :], o["g_down"].at[pl.ds(at, FH), :]))
        self.put(pairs)

    def emit_out(self, value):
        self.refs["g_sq"][0] = value()
        self.put([(self.refs["g_sq"].at[0], self.outs["g_out"])])

    def emit_qkv(self, g, value):
        gs = self.refs["g_sq"]
        gs[0] = value()
        pairs = []
        for c in range(2):
            for k in range(3):
                pairs.append(
                    (gs.at[0, :, pl.ds((c * 3 + k) * 128, 128)], self.outs["g_qkv"].at[k, :, pl.ds((2 * g + c) * 128, 128)])
                )
        self.put(pairs)

    def slot(self, name, j=None):
        pass

    def finish(self):
        self.put([(self.refs["gvec"], self.outs["gvec"])])


def compute(comm, ins, outs, refs):
    r = refs
    h1, qs, ks, vs, ctx = r["h1"], r["qs"], r["ks"], r["vs"], r["ctx"]
    vec, gvec, w4, wup, wdn = r["vec"], r["gvec"], r["w4"], r["wup"], r["wdn"]
    tok, cot, h2, x1, yacc, dh2 = r["tok"], r["cot"], r["h2"], r["x1"], r["yacc"], r["dh2"]
    sem = r["io_sem"]

    load_tok = pltpu.make_async_copy(ins["tokens"], tok, sem.at[0])
    load_ids = pltpu.make_async_copy(ins["ids"], r["idr"], sem.at[1])
    load_cot = pltpu.make_async_copy(ins["cotangent"], cot, sem.at[2])
    load_tok.start()
    load_ids.start()
    comm.begin()
    load_cot.start()
    gvec[...] = jnp.zeros_like(gvec)
    pair = lax.broadcasted_iota(jnp.int32, (256, 256), 0) // DH
    same = pair == lax.broadcasted_iota(jnp.int32, (256, 256), 1) // DH
    r["avg"][...] = jnp.where(same, 1.0 / DH, 0.0).astype(bf16)
    load_ids.wait()
    r["idc"][...] = jnp.broadcast_to(r["idr"][...], (128, T)).T
    load_tok.wait()
    load_cot.wait()

    comm.weights("vec")

    def ln1(rows):
        hat, _ = row_stats(tok[rows, :].astype(f32))
        h1[rows, :] = (hat * vector(vec, "ln1_gain") + vector(vec, "ln1_bias")).astype(bf16)
        add_vector(gvec, "b_down", col_sum(cot[rows, :].astype(f32)))

    rows_loop(ln1)

    for k, (name, raw, low) in enumerate((("q_gain", yacc, qs), ("k_gain", dh2, ks))):
        comm.weights("w4", k)

        def project(rows):
            value = dot(h1[rows, :], w4[k], 1, 0)
            raw[rows, :] = value
            gain = vector(vec, name)
            for b in range(D // 256):
                cols = slice(b * 256, (b + 1) * 256)
                centre = value[:, cols] - head_mean(value[:, cols], r["avg"][...])
                spread = head_mean(centre * centre, r["avg"][...])
                low[rows, cols] = (centre * lax.rsqrt(spread + EPS) * gain[:, cols]).astype(bf16)

        rows_loop(project)
    comm.weights("w4", 2)

    def project_values(rows):
        vs[rows, :] = (dot(h1[rows, :], w4[2], 1, 0) + vector(vec, "b_value")).astype(bf16)

    rows_loop(project_values)
    save = [
        pltpu.make_async_copy(yacc, outs["q_raw"], sem.at[3]),
        pltpu.make_async_copy(dh2, outs["k_raw"], sem.at[4]),
    ]
    for c in save:
        c.start()

    lane = lax.broadcasted_iota(jnp.int32, (1, 128), 1)
    first = lane < DH
    halves = (first, jnp.logical_not(first))
    oacc = r["oacc"]
    ones = jnp.ones((KB, 128), bf16)

    def attend(hp, carry):
        cols = pl.ds(pl.multiple_of(hp * 128, 128), 128)
        oacc[...] = jnp.zeros_like(oacc)
        for j in range(NK):
            lo, hi = max(0, j - 1) * KB, min(NK, j + 2) * KB
            key = ks[j * KB : (j + 1) * KB, cols]
            wide = jnp.concatenate([vs[j * KB : (j + 1) * KB, cols], ones], 1)
            query = qs[lo:hi, cols]
            allowed = r["idc"][lo:hi, 0:1] == r["idr"][:, j * KB : (j + 1) * KB]
            for h in range(2):
                scores = dot(query, jnp.where(halves[h], key, jnp.zeros_like(key)), 1, 1)
                probs = jnp.where(allowed, jnp.exp(scores * SCALE), 0.0).astype(bf16)
                oacc[h, lo:hi, :] += dot(probs, wide, 1, 0)
        inv0 = 1.0 / oacc[0, :, 128:]
        inv1 = 1.0 / oacc[1, :, 128:]
        ctx[:, cols] = jnp.where(first, oacc[0, :, :128] * inv0, oacc[1, :, :128] * inv1).astype(bf16)
        r["inv"][hp] = jnp.where(first, inv0, inv1)
        comm.weights("attend", hp)
        return carry

    lax.fori_loop(0, HEADS // 2, attend, 0)
    for c in save:
        c.wait()

    comm.weights("w4", 3)

    def out_rows(rows):
        value = tok[rows, :].astype(f32) + (dot(ctx[rows, :], w4[3], 1, 0) + vector(vec, "b_out"))
        x1[rows, :] = value
        yacc[rows, :] = value + vector(vec, "b_down")
        dh2[rows, :] = jnp.zeros((RB, D), f32)
        hat, _ = row_stats(value)
        h2[rows, :] = (hat * vector(vec, "ln2_gain") + vector(vec, "ln2_bias")).astype(bf16)

    rows_loop(out_rows)

    act, dpre = r["act"], r["dpre"]

    def chunk(j, carry):
        comm.weights("mlp", j)
        at = pl.multiple_of(VEC["b_up"] + j * FH, 128)
        bias = jnp.concatenate([vec[0, :, pl.ds(at, FH)], vec[1, :, pl.ds(at, FH)]], 1)

        def mlp_rows(rows):
            pre = dot(h2[rows, :], wup[j], 1, 0) + bias
            d_act = dot(cot[rows, :], wdn[j], 1, 1)
            cdf = 0.5 * (1.0 + lax.erf(pre * RSQRT2))
            pdf = jnp.exp(-0.5 * pre * pre) * RSQRT2PI
            low = (pre * cdf).astype(bf16)
            d_low = (d_act * (cdf + pre * pdf)).astype(bf16)
            act[rows, :] = low
            dpre[rows, :] = d_low
            total = col_sum(d_low.astype(f32))
            gvec[0, :, pl.ds(at, FH)] += total[:, :FH]
            gvec[1, :, pl.ds(at, FH)] += total[:, FH:]
            yacc[rows, :] += dot(low, wdn[j], 1, 0)
            dh2[rows, :] += dot(d_low, wup[j], 1, 1)

        rows_loop(mlp_rows)
        comm.slot("mlp", j)
        comm.emit_mlp(
            j,
            lambda: dot(h2[...], dpre[...], 0, 0).astype(bf16),
            lambda: dot(act[...], cot[...], 0, 0).astype(bf16),
        )
        return carry

    lax.fori_loop(0, NJ, chunk, 0)

    low_out = r["low_out"]

    def ln2_back(rows):
        low_out[rows, :] = yacc[rows, :].astype(bf16)
        hat, inv = row_stats(x1[rows, :])
        d_h2 = dh2[rows, :]
        add_vector(gvec, "ln2_gain", col_sum(d_h2 * hat))
        add_vector(gvec, "ln2_bias", col_sum(d_h2))
        scaled = d_h2 * vector(vec, "ln2_gain")
        mean = jnp.mean(scaled, -1, keepdims=True)
        along = jnp.mean(scaled * hat, -1, keepdims=True)
        d_x1 = cot[rows, :].astype(f32) + inv * (scaled - mean - hat * along)
        dh2[rows, :] = d_x1
        d_att = d_x1.astype(bf16)
        h2[rows, :] = d_att
        add_vector(gvec, "b_out", col_sum(d_att.astype(f32)))
        cot[rows, :] = dot(d_att, w4[3], 1, 1).astype(bf16)

    rows_loop(ln2_back)
    store_out = pltpu.make_async_copy(low_out, outs["outputs"], sem.at[5])
    store_out.start()
    comm.slot("ln2")
    comm.emit_out(lambda: dot(ctx[...], h2[...], 0, 0).astype(bf16))
    comm.slot("out")

    d_h1 = x1
    raw_q, raw_k, dqf, dkf, dql = r["raw_q"], r["raw_k"], r["dqf"], r["dkf"], r["dql"]
    for g in range(HEADS // 4):
        gcols = slice(g * 256, (g + 1) * 256)
        back = [
            pltpu.make_async_copy(outs["q_raw"].at[:, pl.ds(g * 256, 256)], raw_q, sem.at[6]),
            pltpu.make_async_copy(outs["k_raw"].at[:, pl.ds(g * 256, 256)], raw_k, sem.at[7]),
        ]
        for c in back:
            c.start()

        def attend_back(p, carry):
            hp = 2 * g + p
            cols = pl.ds(pl.multiple_of(hp * 128, 128), 128)
            local = pl.ds(pl.multiple_of(p * 128, 128), 128)
            vcols = pl.ds(pl.multiple_of(p * 384 + 256, 128), 128)
            product = cot[:, cols].astype(f32) * ctx[:, cols].astype(f32)
            deltas = [jnp.sum(jnp.where(m, product, 0.0), -1, keepdims=True) for m in halves]
            inv = r["inv"][hp]
            invs = (inv[:, 0:1], inv[:, DH : DH + 1])
            dqf[:, local] = jnp.zeros((T, 128), f32)
            for j in range(NK):
                lo, hi = max(0, j - 1) * KB, min(NK, j + 2) * KB
                tile = slice(j * KB, (j + 1) * KB)
                key, value = ks[tile, cols], vs[tile, cols]
                query, d_ctx = qs[lo:hi, cols], cot[lo:hi, cols]
                allowed = r["idc"][lo:hi, 0:1] == r["idr"][:, tile]
                d_keys, d_values = [], []
                for h in range(2):
                    key_h = jnp.where(halves[h], key, jnp.zeros_like(key))
                    value_h = jnp.where(halves[h], value, jnp.zeros_like(value))
                    scores = dot(query, key_h, 1, 1)
                    probs = jnp.where(allowed, jnp.exp(scores * SCALE) * invs[h][lo:hi], 0.0)
                    d_probs = dot(d_ctx, value_h, 1, 1)
                    d_scores = (probs * (d_probs - deltas[h][lo:hi])).astype(bf16)
                    dqf[lo:hi, local] += dot(d_scores, key_h, 1, 0)
                    d_values.append(dot(probs.astype(bf16), d_ctx, 0, 0))
                    d_keys.append(dot(d_scores, query, 0, 0))
                dkf[tile, local] = jnp.where(first, d_keys[0], d_keys[1])
                dql[tile, vcols] = jnp.where(first, d_values[0], d_values[1]).astype(bf16)
            return carry

        lax.fori_loop(0, 2, attend_back, 0)
        comm.slot("att", g)
        for c in back:
            c.wait()

        def heads_back(rows):
            for k, (name, raw, grad) in enumerate((("q_gain", raw_q, dqf), ("k_gain", raw_k, dkf))):
                value = raw[rows, :]
                centre = value - head_mean(value, r["avg"][...])
                inv = lax.rsqrt(head_mean(centre * centre, r["avg"][...]) + EPS)
                hat = centre * inv
                d_low = grad[rows, :] * SCALE
                total = col_sum(d_low * hat)
                gain = vector(vec, name)[:, gcols]
                scaled = d_low * gain
                mean = head_mean(scaled, r["avg"][...])
                along = head_mean(scaled * hat, r["avg"][...])
                d_raw = (inv * (scaled - mean - hat * along)).astype(bf16)
                for c in range(2):
                    dql[rows, (c * 3 + k) * 128 : (c * 3 + k + 1) * 128] = d_raw[:, c * 128 : (c + 1) * 128]
                add_group(gvec, name, g, total)
            d_value = jnp.concatenate([dql[rows, 256:384], dql[rows, 640:768]], 1).astype(f32)
            add_group(gvec, "b_value", g, col_sum(d_value))

        rows_loop(heads_back)
        comm.emit_qkv(g, lambda: dot(h1[...], dql[...], 0, 0).astype(bf16))

        def h1_back(rows):
            total = None
            for k in range(3):
                d_low = jnp.concatenate([dql[rows, (c * 3 + k) * 128 : (c * 3 + k + 1) * 128] for c in range(2)], 1)
                part = dot(d_low, w4[k, :, gcols], 1, 1)
                total = part if total is None else total + part
            if g == 0:
                d_h1[rows, :] = total
            else:
                d_h1[rows, :] += total

        if g == 0:
            store_out.wait()
            again = pltpu.make_async_copy(ins["tokens"], tok, sem.at[0])
            again.start()
        rows_loop(h1_back)
        comm.slot("qkv", g)

    again.wait()

    def ln1_back(rows):
        hat, inv = row_stats(tok[rows, :].astype(f32))
        grad = d_h1[rows, :]
        add_vector(gvec, "ln1_gain", col_sum(grad * hat))
        add_vector(gvec, "ln1_bias", col_sum(grad))
        scaled = grad * vector(vec, "ln1_gain")
        mean = jnp.mean(scaled, -1, keepdims=True)
        along = jnp.mean(scaled * hat, -1, keepdims=True)
        low_out[rows, :] = (dh2[rows, :] + inv * (scaled - mean - hat * along)).astype(bf16)

    rows_loop(ln1_back)
    store_tok = pltpu.make_async_copy(low_out, outs["d_tokens"], sem.at[5])
    store_tok.start()
    comm.finish()
    store_tok.wait()


def add_group(gvec, name, g, total):
    for c in range(2):
        col = g * 256 + c * 128
        at = VEC[name] + col % HD
        gvec[col // HD, :, at : at + 128] += total[:, c * 128 : (c + 1) * 128]


def scratch_common():
    vm = pltpu.VMEM
    return dict(
        w4=vm((4, D, D), bf16),
        wup=vm((NJ, D, FC), bf16),
        wdn=vm((NJ, FC, D), bf16),
        vec=vm((2, 1, NV), f32),
        gvec=vm((2, 1, NV), f32),
        avg=vm((256, 256), bf16),
        idr=vm((1, T), jnp.int32),
        idc=vm((T, 128), jnp.int32),
        tok=vm((T, D), bf16),
        cot=vm((T, D), bf16),
        h1=vm((T, D), bf16),
        qs=vm((T, D), bf16),
        ks=vm((T, D), bf16),
        vs=vm((T, D), bf16),
        ctx=vm((T, D), bf16),
        inv=vm((HEADS // 2, T, 128), f32),
        x1=vm((T, D), f32),
        h2=vm((T, D), bf16),
        yacc=vm((T, D), f32),
        dh2=vm((T, D), f32),
        low_out=vm((T, D), bf16),
        act=vm((T, FC), bf16),
        dpre=vm((T, FC), bf16),
        oacc=vm((2, T, 256), f32),
        raw_q=vm((T, 256), f32),
        raw_k=vm((T, 256), f32),
        dqf=vm((T, 256), f32),
        dkf=vm((T, 256), f32),
        dql=vm((T, D), bf16),
        io_sem=pltpu.SemaphoreType.DMA((8,)),
    )


def scratch_plain():
    vm = pltpu.VMEM
    return dict(
        scratch_common(),
        g_up=vm((1, D, FC), bf16),
        g_dn=vm((1, FC, D), bf16),
        g_sq=vm((1, D, D), bf16),
        load_sem=pltpu.SemaphoreType.DMA((32,)),
    )


IN_NAMES = ("tokens", "ids", "cotangent", "w_query", "w_key", "w_value", "w_out", "w_up", "w_down", "vec")


def run_kernel(make_comm, out_shapes, scratch, args, params):
    out_names, scratch_names = tuple(out_shapes), tuple(scratch)

    def kernel(*all_refs):
        n_in, n_out = len(IN_NAMES), len(out_names)
        ins = dict(zip(IN_NAMES, all_refs[:n_in]))
        outs = dict(zip(out_names, all_refs[n_in : n_in + n_out]))
        refs = dict(zip(scratch_names, all_refs[n_in + n_out :]))
        compute(make_comm(ins, outs, refs), ins, outs, refs)

    anywhere = pl.BlockSpec(memory_space=pl.ANY)
    result = pl.pallas_call(
        kernel,
        out_shape=tuple(out_shapes.values()),
        in_specs=[anywhere] * len(IN_NAMES),
        out_specs=(anywhere,) * len(out_names),
        scratch_shapes=list(scratch.values()),
        compiler_params=params,
        name="encoder_layer",
    )(*[args[n] for n in IN_NAMES])
    return dict(zip(out_names, result))


def shape(dims, dtype):
    return jax.ShapeDtypeStruct(dims, dtype)


VECTORS = ("ln1_gain", "ln1_bias", "b_value", "q_gain", "k_gain", "b_out", "ln2_gain", "ln2_bias", "b_down", "b_up")


def plain_layer(a):
    def whole(value):
        return lax.all_gather(value, "shard", axis=0, tiled=True)

    args = dict(tokens=a["tokens"], ids=a["image_ids"], cotangent=a["cotangent"])
    for n in ("w_query", "w_key", "w_value", "w_out", "w_up", "w_down"):
        args[n] = whole(a[n])
    vecs = [whole(a[n]).astype(f32).reshape(2, -1) for n in VECTORS]
    args["vec"] = jnp.concatenate(vecs, 1).reshape(2, 1, NV)
    out_shapes = dict(
        outputs=shape((T, D), bf16),
        d_tokens=shape((T, D), bf16),
        g_up=shape((D, FF), bf16),
        g_down=shape((FF, D), bf16),
        g_out=shape((D, D), bf16),
        g_qkv=shape((3, D, D), bf16),
        gvec=shape((2, 1, NV), f32),
        q_raw=shape((T, D), f32),
        k_raw=shape((T, D), f32),
    )
    params = pltpu.CompilerParams(vmem_limit_bytes=67043328)
    o = run_kernel(Plain, out_shapes, scratch_plain(), args, params)

    def reduce(value):
        part = lax.psum_scatter(value.astype(f32), "shard", scatter_dimension=0, tiled=True)
        return lax.psum(part, "rep")

    grads = dict(w_out=o["g_out"], w_up=o["g_up"], w_down=o["g_down"])
    for k, n in enumerate(("w_query", "w_key", "w_value")):
        grads[n] = o["g_qkv"][k]
    gvec = o["gvec"].reshape(2, NV)
    for n in VECTORS:
        at = VEC[n]
        size = HF if n == "b_up" else HD
        grads[n] = gvec[:, at : at + size].reshape(-1)
    grads = {n: reduce(v) for n, v in grads.items()}
    return o["outputs"], o["d_tokens"], grads


ARGS = (
    "tokens",
    "image_ids",
    "ln1_gain",
    "ln1_bias",
    "w_query",
    "w_key",
    "w_value",
    "b_value",
    "q_gain",
    "k_gain",
    "w_out",
    "b_out",
    "ln2_gain",
    "ln2_bias",
    "w_up",
    "b_up",
    "w_down",
    "b_down",
    "cotangent",
)


def specs(names):
    both = P(("rep", "shard"), None)
    table = dict(tokens=both, image_ids=both, cotangent=both)
    return tuple(table.get(n, P("shard", None) if n.startswith("w_") else P("shard")) for n in names)


def solution(mesh):
    def on_device(*values):
        outputs, d_tokens, grads = plain_layer(dict(zip(ARGS, values)))
        return (outputs, d_tokens) + tuple(grads[n] for n in ARGS[2:-1])

    both = P(("rep", "shard"), None)
    return jax.shard_map(
        on_device,
        mesh=mesh,
        in_specs=specs(ARGS),
        out_specs=(both, both) + specs(ARGS[2:-1]),
        check_vma=False,
    )
```
